32 devices in a mesh: rows: 8 (over z, x), grp: 4 (over y, core).
Axes of the slice: x: 2, y: 2, z: 4, core: 2. Of those that a mesh axis runs over, the one named last changes fastest.
Arguments:
- matrix: float32 [65536, 1024], P(('rows', 'grp'))
- row_signs: int32 [65536], P(('rows', 'grp')), may hold values from -1 to 1, as said below
- samples: int32 [8192], P(('rows', 'grp')), may hold values from 0 to 65535, as said below
Outputs:
- factor: float32 [1024, 1024], P('rows')
The draws below stay inside these ranges and needn't reach their ends.
Inputs may be any that keep to these rules, and one draw needn't show every extreme that they name: `row_signs`: every entry is 1 or -1. `samples`: entries are distinct and increasing; entries k * 256 to (k + 1) * 256 - 1 lie in rows k * 2048 to (k + 1) * 2048 - 1.
All inputs are finite; a program needn't handle non-finite values.
Results may differ from the reference program's by a relative error of at most 0.00011.
Values sent between devices are 32-bit elements; how exact they have to be, the bound alone decides.
A program may use at most 128 MiB of HBM per device.

```python
import jax
import jax.numpy as jnp
from jax import lax

COLS = 1024
ROW_DEV = 2048
SAMPLES = 8192
ROWS_TOTAL = 65536


def draw_matrix(key, part):
    key_noise = jax.random.fold_in(key, 11)
    key_common = jax.random.fold_in(key, 12)
    key_cols = jax.random.fold_in(key, 13)
    col_scale = jnp.exp(jax.random.uniform(key_cols, (COLS,), jnp.float32, jnp.log(0.5), jnp.log(4.0)))
    noise = jax.random.normal(key_noise, (ROWS_TOTAL, COLS), jnp.float32)
    common = jax.random.normal(key_common, (ROWS_TOTAL, 1), jnp.float32)
    mixed_rows = noise + 0.5 * jnp.roll(noise, 1, axis=1) + 0.6 * common
    return (mixed_rows * col_scale[None, :] / jnp.sqrt(jnp.float32(ROWS_TOTAL))).astype(jnp.float32)


def draw_row_signs(key, part):
    coin_key = jax.random.fold_in(key, 21)
    return (2 * jax.random.randint(coin_key, (ROWS_TOTAL,), 0, 2) - 1).astype(jnp.int32)


def draw_samples(key, part):
    pick_key = jax.random.fold_in(key, 31)
    block_count = ROWS_TOTAL // ROW_DEV
    per_block = SAMPLES // block_count
    block_keys = jax.random.split(pick_key, block_count)
    picks = jax.vmap(lambda one_key: jnp.sort(jax.random.permutation(one_key, ROW_DEV)[:per_block]))(block_keys)
    offsets = ROW_DEV * jnp.arange(block_count, dtype=jnp.int32)[:, None]
    return (picks.astype(jnp.int32) + offsets).reshape(block_count * per_block).astype(jnp.int32)


def setup_inputs(seed: int = 0) -> dict:
    keys = jax.random.split(jax.random.key(seed), 4)
    return {
        "matrix": draw_matrix(jax.random.fold_in(keys[3], 71), 0),
        "row_signs": draw_row_signs(jax.random.fold_in(keys[3], 71), 0),
        "samples": draw_samples(jax.random.fold_in(keys[3], 71), 0),
    }


def walsh_transform(values):
    length, width_cols = values.shape
    half_span = 1
    for section_level in range(length.bit_length() - 1):
        paired = values.reshape(length // (2 * half_span), 2, half_span, width_cols)
        values = jnp.stack([paired[:, 0] + paired[:, 1], paired[:, 0] - paired[:, 1]], axis=1).reshape(length, width_cols)
        half_span = half_span * 2
    return values

def reference(matrix, row_signs, samples):
    total_rows = matrix.shape[0]
    signed = matrix * row_signs.astype(jnp.float32)[:, None]
    transformed = walsh_transform(signed) / jnp.sqrt(jnp.float32(total_rows))
    sampled = transformed[samples] * jnp.sqrt(jnp.float32(total_rows / SAMPLES))
    gram_total = jnp.dot(sampled.T, sampled, precision=lax.Precision.HIGHEST)
    lower_factor = jnp.linalg.cholesky(gram_total)
    return lower_factor.T
```

```python
import functools

import jax
import jax.numpy as jnp
from jax import lax
from jax.experimental import pallas as pl
from jax.experimental.pallas import tpu as pltpu
from jax.sharding import PartitionSpec as P

exact_mode = lax.Precision.HIGHEST
VMEM_LIMIT = 60 * 1024 * 1024
TILE = 128


def sylvester(length):
    matrix = jnp.ones((1, 1), jnp.float32)
    while matrix.shape[0] < length:
        matrix = jnp.block([[matrix, matrix], [matrix, -matrix]])
    return matrix


def butterfly(parts):
    span = 1
    while span < len(parts):
        parts = list(parts)
        for start in range(0, len(parts), 2 * span):
            for i in range(start, start + span):
                low, high = parts[i], parts[i + span]
                parts[i], parts[i + span] = low + high, low - high
        span *= 2
    return parts


def split(x):
    high = x.astype(jnp.bfloat16)
    return high, (x - high.astype(jnp.float32)).astype(jnp.bfloat16)


def local_kernel(base, x_ref, s_ref, h_ref, o_ref):
    parts = []
    for i in range(x_ref.shape[0] // base):
        rows = slice(i * base, (i + 1) * base)
        high, low = split(x_ref[rows, :] * s_ref[rows, :])
        both = jnp.dot(h_ref[...], high, preferred_element_type=jnp.float32)
        both += jnp.dot(h_ref[...], low, preferred_element_type=jnp.float32)
        parts.append(both)
    for i, part in enumerate(butterfly(parts)):
        o_ref[i * base : (i + 1) * base, :] = part


def local_transform(matrix, signs, base):
    rows, cols = matrix.shape
    return pl.pallas_call(
        functools.partial(local_kernel, base),
        grid=(cols // TILE,),
        out_shape=jax.ShapeDtypeStruct((rows, cols), jnp.float32),
        in_specs=[
            pl.BlockSpec((rows, TILE), lambda c: (0, c)),
            pl.BlockSpec((rows, TILE), lambda c: (0, 0)),
            pl.BlockSpec((base, base), lambda c: (0, 0)),
        ],
        out_specs=pl.BlockSpec((rows, TILE), lambda c: (0, c)),
        compiler_params=pltpu.CompilerParams(vmem_limit_bytes=VMEM_LIMIT),
    )(matrix, signs, sylvester(base).astype(jnp.bfloat16))


def gram_kernel(scale, x_ref, w_ref, o_ref, left, right):
    blocks, step, cols = x_ref.shape
    rows = blocks * step

    @pl.when(pl.program_id(0) == 0)
    def _():
        o_ref[...] = jnp.zeros_like(o_ref)

    def mix(c, carry):
        at = pl.ds(pl.multiple_of(c * TILE, TILE), TILE)
        parts = butterfly([x_ref[b, :, at] for b in range(blocks)])
        for b in range(0, blocks, 2):
            x = jnp.concatenate(parts[b : b + 2], axis=0) * scale
            w = jnp.concatenate([w_ref[b], w_ref[b + 1]], axis=0)
            high, low = split(x)
            here = slice(b * step, (b + 2) * step)
            there = slice(rows + b * step, rows + (b + 2) * step)
            masked = (high.astype(jnp.float32) * w).astype(jnp.bfloat16)
            left[here, at] = masked
            right[here, at] = high
            left[there, at] = masked
            right[there, at] = (2.0 * low.astype(jnp.float32)).astype(jnp.bfloat16)
        return carry

    lax.fori_loop(0, cols // TILE, mix, 0)
    wide = 2 * TILE

    def add(n, carry):
        at = pl.ds(pl.multiple_of(n * wide, wide), wide)
        o_ref[:, at] += lax.dot_general(
            left[...], right[:, at], (((0,), (0,)), ((), ())), preferred_element_type=jnp.float32
        )
        return carry

    lax.fori_loop(0, cols // wide, add, 0)


def gram_share(arrived, weights, scale):
    blocks, piece, cols = arrived.shape
    step = 8
    return pl.pallas_call(
        functools.partial(gram_kernel, scale),
        grid=(piece // step,),
        out_shape=jax.ShapeDtypeStruct((cols, cols), jnp.float32),
        in_specs=[
            pl.BlockSpec((blocks, step, cols), lambda t: (0, t, 0)),
            pl.BlockSpec((blocks, step, TILE), lambda t: (0, t, 0)),
        ],
        out_specs=pl.BlockSpec((cols, cols), lambda t: (0, 0)),
        scratch_shapes=[pltpu.VMEM((2 * blocks * step, cols), jnp.bfloat16)] * 2,
        compiler_params=pltpu.CompilerParams(vmem_limit_bytes=VMEM_LIMIT),
    )(arrived, weights)


def factor_kernel(g_ref, u_ref, work):
    cols = g_ref.shape[0]
    work[...] = g_ref[...]
    row_id = lax.broadcasted_iota(jnp.int32, (TILE, TILE), 0)
    lane_id = lax.broadcasted_iota(jnp.int32, (TILE, TILE), 1)

    def panel(k, carry):
        base = pl.multiple_of(k * TILE, TILE)
        here = pl.ds(base, TILE)
        block = work[here, here]
        strips = [block[i : i + 8, :] for i in range(0, TILE, 8)]
        unit = (row_id == lane_id).astype(jnp.float32)
        inverse = [unit[i : i + 8, :] for i in range(0, TILE, 8)]
        sub_id = lax.broadcasted_iota(jnp.int32, (8, TILE), 0)
        for j in range(TILE):
            s, r = divmod(j, 8)
            row = strips[s][r : r + 1, :]
            inv_row = inverse[s][r : r + 1, :]
            root = lax.rsqrt(jnp.broadcast_to(row[:, j : j + 1], (1, TILE)))
            row = row * root
            inv_row = inv_row * root
            for i in range(s, TILE // 8):
                column = jnp.broadcast_to(strips[i][:, j : j + 1], (8, TILE)) * root
                if i == s:
                    column = jnp.where(sub_id > r, column, 0.0)
                strips[i] = strips[i] - column * row
                inverse[i] = inverse[i] - column * inv_row
                if i == s:
                    inverse[i] = jnp.where(sub_id == r, inv_row, inverse[i])
        lower_inverse = jnp.concatenate(inverse, axis=0)
        lower_inverse = jnp.where(lane_id <= row_id, lower_inverse, 0.0)
        wide_row = lax.broadcasted_iota(jnp.int32, (TILE, cols), 0) + base
        wide_lane = lax.broadcasted_iota(jnp.int32, (TILE, cols), 1)
        upper = jnp.dot(
            lower_inverse, work[here, :], precision=exact_mode, preferred_element_type=jnp.float32
        )
        u_ref[here, :] = jnp.where(wide_lane >= wide_row, upper, 0.0)

        def trail(i, inner):
            there = pl.ds(pl.multiple_of(i * TILE, TILE), TILE)
            work[there, :] -= lax.dot_general(
                u_ref[here, there],
                u_ref[here, :],
                (((0,), (0,)), ((), ())),
                precision=exact_mode,
                preferred_element_type=jnp.float32,
            )
            return inner

        lax.fori_loop(k + 1, cols // TILE, trail, 0)
        return carry

    lax.fori_loop(0, cols // TILE, panel, 0)


def factorize(gram):
    return pl.pallas_call(
        factor_kernel,
        out_shape=jax.ShapeDtypeStruct(gram.shape, jnp.float32),
        in_specs=[pl.BlockSpec(memory_space=pltpu.VMEM)],
        out_specs=pl.BlockSpec(memory_space=pltpu.VMEM),
        scratch_shapes=[pltpu.VMEM(gram.shape, jnp.float32)],
        compiler_params=pltpu.CompilerParams(vmem_limit_bytes=VMEM_LIMIT),
    )(gram)


def shards(matrix, row_signs, samples):
    count_rows = lax.axis_size("rows")
    blocks = count_rows * lax.axis_size("grp")
    row_dev, col_count = matrix.shape
    piece_rows = row_dev // blocks
    sample_dev = samples.shape[0]
    position = lax.axis_index(("rows", "grp"))
    all_indices = lax.all_gather(samples, ("rows", "grp"), axis=0)
    signs = jnp.broadcast_to(row_signs.astype(jnp.float32)[:, None], (row_dev, TILE))
    before = local_transform(matrix, signs, min(256, row_dev))
    arrived = lax.all_to_all(
        before.reshape(blocks, piece_rows, col_count),
        ("rows", "grp"),
        split_axis=0,
        concat_axis=0,
        tiled=True,
    )
    first = jnp.arange(blocks, dtype=jnp.int32)[:, None] * row_dev + position * piece_rows
    within = all_indices - first
    hits = within[:, None, :] == jnp.arange(piece_rows, dtype=jnp.int32)[None, :, None]
    weights = jnp.max(hits.astype(jnp.float32), axis=2)
    weights = jnp.broadcast_to(weights[:, :, None], (blocks, piece_rows, TILE))
    scale = (sample_dev * blocks) ** -0.5
    half = gram_share(arrived, weights, scale)
    summed = lax.psum((half + half.T) * 0.5, ("rows", "grp"))
    upper_factor = factorize(summed)
    share_rows = col_count // count_rows
    return lax.dynamic_slice_in_dim(
        upper_factor, lax.axis_index("rows") * share_rows, share_rows, 0
    )


def solution(mesh):
    return jax.shard_map(
        shards,
        mesh=mesh,
        in_specs=(P(("rows", "grp"), None), P(("rows", "grp")), P(("rows", "grp"))),
        out_specs=P("rows", None),
        check_vma=False,
    )
```

```python
import functools

import jax
import jax.numpy as jnp
from jax import lax
from jax.experimental import pallas as pl
from jax.experimental.pallas import tpu as pltpu
from jax.sharding import PartitionSpec as P

exact_mode = lax.Precision.HIGHEST
VMEM_LIMIT = 60 * 1024 * 1024
TILE = 128


def sylvester(length):
    matrix = jnp.ones((1, 1), jnp.float32)
    while matrix.shape[0] < length:
        matrix = jnp.block([[matrix, matrix], [matrix, -matrix]])
    return matrix


def butterfly(parts):
    span = 1
    while span < len(parts):
        parts = list(parts)
        for start in range(0, len(parts), 2 * span):
            for i in range(start, start + span):
                low, high = parts[i], parts[i + span]
                parts[i], parts[i + span] = low + high, low - high
        span *= 2
    return parts


def split(x):
    high = x.astype(jnp.bfloat16)
    return high, (x - high.astype(jnp.float32)).astype(jnp.bfloat16)


def local_kernel(base, x_ref, s_ref, h_ref, o_ref):
    parts = []
    for i in range(x_ref.shape[0] // base):
        rows = slice(i * base, (i + 1) * base)
        high, low = split(x_ref[rows, :] * s_ref[rows, :])
        both = jnp.dot(h_ref[...], high, preferred_element_type=jnp.float32)
        both += jnp.dot(h_ref[...], low, preferred_element_type=jnp.float32)
        parts.append(both)
    for i, part in enumerate(butterfly(parts)):
        o_ref[i * base : (i + 1) * base, :] = part


def local_transform(matrix, signs, base):
    rows, cols = matrix.shape
    return pl.pallas_call(
        functools.partial(local_kernel, base),
        grid=(cols // TILE,),
        out_shape=jax.ShapeDtypeStruct((rows, cols), jnp.float32),
        in_specs=[
            pl.BlockSpec((rows, TILE), lambda c: (0, c)),
            pl.BlockSpec((rows, TILE), lambda c: (0, 0)),
            pl.BlockSpec((base, base), lambda c: (0, 0)),
        ],
        out_specs=pl.BlockSpec((rows, TILE), lambda c: (0, c)),
        compiler_params=pltpu.CompilerParams(vmem_limit_bytes=VMEM_LIMIT),
    )(matrix, signs, sylvester(base).astype(jnp.bfloat16))


def gram_kernel(scale, x_ref, w_ref, o_ref, left, right):
    blocks, step, cols = x_ref.shape
    rows = blocks * step

    @pl.when(pl.program_id(0) == 0)
    def _():
        o_ref[...] = jnp.zeros_like(o_ref)

    def mix(c, carry):
        at = pl.ds(pl.multiple_of(c * TILE, TILE), TILE)
        parts = butterfly([x_ref[b, :, at] for b in range(blocks)])
        for b in range(0, blocks, 2):
            x = jnp.concatenate(parts[b : b + 2], axis=0) * scale
            w = jnp.concatenate([w_ref[b], w_ref[b + 1]], axis=0)
            high, low = split(x)
            here = slice(b * step, (b + 2) * step)
            there = slice(rows + b * step, rows + (b + 2) * step)
            masked = (high.astype(jnp.float32) * w).astype(jnp.bfloat16)
            left[here, at] = masked
            right[here, at] = high
            left[there, at] = masked
            right[there, at] = (2.0 * low.astype(jnp.float32)).astype(jnp.bfloat16)
        return carry

    lax.fori_loop(0, cols // TILE, mix, 0)
    wide = 2 * TILE

    def add(n, carry):
        at = pl.ds(pl.multiple_of(n * wide, wide), wide)
        o_ref[:, at] += lax.dot_general(
            left[...], right[:, at], (((0,), (0,)), ((), ())), preferred_element_type=jnp.float32
        )
        return carry

    lax.fori_loop(0, cols // wide, add, 0)


def gram_share(arrived, weights, scale):
    blocks, piece, cols = arrived.shape
    step = 8
    return pl.pallas_call(
        functools.partial(gram_kernel, scale),
        grid=(piece // step,),
        out_shape=jax.ShapeDtypeStruct((cols, cols), jnp.float32),
        in_specs=[
            pl.BlockSpec((blocks, step, cols), lambda t: (0, t, 0)),
            pl.BlockSpec((blocks, step, TILE), lambda t: (0, t, 0)),
        ],
        out_specs=pl.BlockSpec((cols, cols), lambda t: (0, 0)),
        scratch_shapes=[pltpu.VMEM((2 * blocks * step, cols), jnp.bfloat16)] * 2,
        compiler_params=pltpu.CompilerParams(vmem_limit_bytes=VMEM_LIMIT),
    )(arrived, weights)


def upper_tiles(cols):
    return [(i, j) for i in range(0, cols, TILE) for j in range(i, cols, TILE)]


def factor_kernel(g_ref, u_ref, work):
    cols = u_ref.shape[0]
    work[...] = jnp.zeros_like(work)
    for p, (i, j) in enumerate(upper_tiles(cols)):
        work[i : i + TILE, j : j + TILE] = g_ref[p * TILE : (p + 1) * TILE, :]
    row_id = lax.broadcasted_iota(jnp.int32, (TILE, TILE), 0)
    lane_id = lax.broadcasted_iota(jnp.int32, (TILE, TILE), 1)

    def panel(k, carry):
        base = pl.multiple_of(k * TILE, TILE)
        here = pl.ds(base, TILE)
        block = work[here, here]
        strips = [block[i : i + 8, :] for i in range(0, TILE, 8)]
        unit = (row_id == lane_id).astype(jnp.float32)
        inverse = [unit[i : i + 8, :] for i in range(0, TILE, 8)]
        sub_id = lax.broadcasted_iota(jnp.int32, (8, TILE), 0)
        for j in range(TILE):
            s, r = divmod(j, 8)
            row = strips[s][r : r + 1, :]
            inv_row = inverse[s][r : r + 1, :]
            root = lax.rsqrt(jnp.broadcast_to(row[:, j : j + 1], (1, TILE)))
            row = row * root
            inv_row = inv_row * root
            for i in range(s, TILE // 8):
                column = jnp.broadcast_to(strips[i][:, j : j + 1], (8, TILE)) * root
                if i == s:
                    column = jnp.where(sub_id > r, column, 0.0)
                strips[i] = strips[i] - column * row
                inverse[i] = inverse[i] - column * inv_row
                if i == s:
                    inverse[i] = jnp.where(sub_id == r, inv_row, inverse[i])
        lower_inverse = jnp.concatenate(inverse, axis=0)
        lower_inverse = jnp.where(lane_id <= row_id, lower_inverse, 0.0)
        wide_row = lax.broadcasted_iota(jnp.int32, (TILE, cols), 0) + base
        wide_lane = lax.broadcasted_iota(jnp.int32, (TILE, cols), 1)
        upper = jnp.dot(
            lower_inverse, work[here, :], precision=exact_mode, preferred_element_type=jnp.float32
        )
        u_ref[here, :] = jnp.where(wide_lane >= wide_row, upper, 0.0)

        def trail(i, inner):
            there = pl.ds(pl.multiple_of(i * TILE, TILE), TILE)
            work[there, :] -= lax.dot_general(
                u_ref[here, there],
                u_ref[here, :],
                (((0,), (0,)), ((), ())),
                precision=exact_mode,
                preferred_element_type=jnp.float32,
            )
            return inner

        lax.fori_loop(k + 1, cols // TILE, trail, 0)
        return carry

    lax.fori_loop(0, cols // TILE, panel, 0)


def factorize(packed, cols):
    return pl.pallas_call(
        factor_kernel,
        out_shape=jax.ShapeDtypeStruct((cols, cols), jnp.float32),
        in_specs=[pl.BlockSpec(memory_space=pltpu.VMEM)],
        out_specs=pl.BlockSpec(memory_space=pltpu.VMEM),
        scratch_shapes=[pltpu.VMEM((cols, cols), jnp.float32)],
        compiler_params=pltpu.CompilerParams(vmem_limit_bytes=VMEM_LIMIT),
    )(packed)


def shards(matrix, row_signs, samples):
    count_rows = lax.axis_size("rows")
    blocks = count_rows * lax.axis_size("grp")
    row_dev, col_count = matrix.shape
    piece_rows = row_dev // blocks
    sample_dev = samples.shape[0]
    position = lax.axis_index(("rows", "grp"))
    all_indices = lax.all_gather(samples, ("rows", "grp"), axis=0)
    signs = jnp.broadcast_to(row_signs.astype(jnp.float32)[:, None], (row_dev, TILE))
    before = local_transform(matrix, signs, min(256, row_dev))
    arrived = lax.all_to_all(
        before.reshape(blocks, piece_rows, col_count),
        ("rows", "grp"),
        split_axis=0,
        concat_axis=0,
        tiled=True,
    )
    first = jnp.arange(blocks, dtype=jnp.int32)[:, None] * row_dev + position * piece_rows
    within = all_indices - first
    hits = within[:, None, :] == jnp.arange(piece_rows, dtype=jnp.int32)[None, :, None]
    weights = jnp.max(hits.astype(jnp.float32), axis=2)
    weights = jnp.broadcast_to(weights[:, :, None], (blocks, piece_rows, TILE))
    scale = (sample_dev * blocks) ** -0.5
    half = gram_share(arrived, weights, scale)
    whole = (half + half.T) * 0.5
    packed = jnp.concatenate(
        [whole[i : i + TILE, j : j + TILE] for i, j in upper_tiles(col_count)], axis=0
    )
    summed = lax.psum(packed, ("rows", "grp"))
    upper_factor = factorize(summed, col_count)
    share_rows = col_count // count_rows
    return lax.dynamic_slice_in_dim(
        upper_factor, lax.axis_index("rows") * share_rows, share_rows, 0
    )


def solution(mesh):
    return jax.shard_map(
        shards,
        mesh=mesh,
        in_specs=(P(("rows", "grp"), None), P(("rows", "grp")), P(("rows", "grp"))),
        out_specs=P("rows", None),
        check_vma=False,
    )
```
